512 devices in a mesh: wide: 64 (over x, z, core), narrow: 8 (over y).
Axes of the slice: x: 4, y: 8, z: 8, core: 2. Of those that a mesh axis runs over, the one named last changes fastest.
Arguments:
- quot_owner: int32 [262144, 1], P(('wide', 'narrow')), may hold values from 0 to 63; in each aligned block of 512 rows (0 to 511, 512 to 1023, ...) at most 16 rows name the same one
- quot_row: int32 [262144], P(('wide', 'narrow')), may hold values from 0 to 1023
- rem_owner: int32 [262144, 1], P(('wide', 'narrow')), may hold values from 0 to 7, as said below
- rem_row: int32 [262144], P(('wide', 'narrow')), may hold values from 0 to 4095, as said below
- out_grad: bfloat16 [262144, 256], P(('wide', 'narrow')), may hold values from -6 to 6
- quot_table: bfloat16 [65536, 256], P('wide'), may hold values from -127 to 127
- quot_scale: float32 [65536], P('wide'), may hold values from 0.002 to 0.02
- rem_table: bfloat16 [32768, 256], P('narrow'), may hold values from -4 to 4
Outputs:
- grad_quot: float32 [65536, 256], P('wide')
- grad_rem: float32 [8, 4096, 256], P('narrow', 'wide')
The draws below stay inside these ranges and needn't reach their ends.
Inputs may be any that keep to these rules, and one draw needn't show every extreme that they name: `quot_owner`: of the ids of one device, at most 16 have the same quotient owner, and some device reaches it. `rem_owner`: of the ids of one device, exactly 64 have each remainder owner. Of the ids of one device with the same remainder owner, at most 2 have the same rem_row // 64; for one owner and one such block, drawn from the seed, every device has exactly 2.
All inputs are finite; a program needn't handle non-finite values.
Results may differ from the reference program's by a relative error of at most 0.0041.
Values may be sent and summed in bfloat16 or wider, within the bound.
A program may use at most 64 MiB of HBM per device.

```python
import math
import jax
import jax.numpy as jnp
import numpy as np

E = 256
QROWS = 65536
RROWS = 32768
TOK_DEV = 512
TOKENS = 262144
QPER = 1024
RPER = 4096
CAPQ = 16
CAPR = 64
CAPB = 2
N_WIDE = 64
N_NARROW = 8
DEVICES = 512


def remainder_layout(key):
    base = jax.random.fold_in(key, 11)
    chosen = jax.random.fold_in(key, 13)
    star_owner = jax.random.randint(chosen, (), 0, N_NARROW)
    star_block = jax.random.randint(jax.random.fold_in(chosen, 1), (), 0, N_WIDE)
    block_rows = RPER // N_WIDE
    device_keys = jax.random.split(base, DEVICES)

    def one_device(device_key):
        first, second, third = jax.random.split(device_key, 3)
        order = jax.random.permutation(first, TOK_DEV).astype(jnp.int32)
        owner = order // CAPR
        within = order % CAPR
        scores = jax.random.randint(second, (N_NARROW, N_WIDE), 0, 1 << 20) * N_WIDE + jnp.arange(N_WIDE, dtype=jnp.int32)[None, :]
        forced = (jnp.arange(N_NARROW, dtype=jnp.int32)[:, None] == star_owner) & (jnp.arange(N_WIDE, dtype=jnp.int32)[None, :] == star_block)
        scores = jnp.where(forced, -1, scores)
        ranking = jnp.argsort(scores, axis=1).astype(jnp.int32)
        block = ranking[owner, within // CAPB]
        offset = jax.random.randint(third, (TOK_DEV,), 0, block_rows)
        return (owner, (block * block_rows + offset).astype(jnp.int32))
    owners, rows = jax.vmap(one_device)(device_keys)
    return (owners.reshape(TOKENS, 1).astype(jnp.int32), rows.reshape(TOKENS).astype(jnp.int32))


def draw_rem_owner(key, part):
    return remainder_layout(key)[0]


def draw_rem_row(key, part):
    return remainder_layout(key)[1]


def draw_quot_table(key, part):
    codes = jax.random.randint(jax.random.fold_in(key, 5), (QROWS, E), -127, 128)
    return codes.astype(jnp.float32).astype(jnp.bfloat16)


def touch_ends(values, key, least, high):
    spot = [jax.random.randint(jax.random.fold_in(key, axis), (), 0, length) for axis, length in enumerate(values.shape)]
    main_axis = values.shape.index(max(values.shape))
    next_to = spot[:main_axis] + [(spot[main_axis] + 1) % values.shape[main_axis]] + spot[main_axis + 1:]
    return values.at[tuple(spot)].set(least).at[tuple(next_to)].set(high)


def block_scale(key, dims, pieces, smallest, high):
    def one(dim, shards_of):
        draws = jax.random.uniform(jax.random.fold_in(jax.random.fold_in(key, 6), dim), (shards_of,), jnp.float32, smallest / len(pieces), high / len(pieces))
        return jnp.repeat(jnp.exp(draws), dims[dim] // shards_of).reshape((-1,) + (1,) * (len(dims) - dim - 1))

    factor_of = one(*pieces[0])
    for cut in pieces[1:]:
        factor_of = factor_of * one(*cut)
    return factor_of


def cumulative_ranks(amount, slope):
    portions = [(1 << 20) // math.isqrt(grade ** slope) + 1 for grade in range(1, amount + 1)]
    width = 1 + sum(portions) // (1 << 30)
    return np.cumsum(np.array([max(1, weight // width) for weight in portions]))


def ranked(stream_key, dims, count, lean):
    grid = cumulative_ranks(count, lean)
    lot = jax.random.randint(jax.random.fold_in(stream_key, 1), dims, 0, int(grid[count - 1]))
    grade = jnp.searchsorted(jnp.asarray(grid, jnp.int32), lot, side="right")
    return jax.random.permutation(jax.random.fold_in(stream_key, 2), count)[grade].astype(jnp.int32)


def assign_block(own_key, own, number, rows, amount, top, reach, slope):
    order = jax.random.permutation(own_key, amount)
    heavy_load, common = shares(amount, rows * top, reach, slope, True), shares(amount, rows * top, reach, slope, False)
    places = jnp.arange(amount)

    def named(tallies, offset_by):
        used = int((tallies > 0).sum())
        fixed = max(1, used // 4)
        passed = fixed + (places - fixed + offset_by * (used - fixed)) % max(1, amount - fixed)
        return jnp.zeros((amount,), jnp.int32).at[order[jnp.where(places < fixed, places, passed)]].set(jnp.asarray(tallies, jnp.int32))

    tallies = jnp.where(number % 4 == 0, named(heavy_load, number // 4), named(common, number - number // 4 - 1))
    mixed = jax.random.permutation(jax.random.fold_in(own, 3), amount)
    giver, taker = mixed[0:amount // 2 * 2:2], mixed[1:amount // 2 * 2:2]
    margin = jnp.minimum(tallies[giver] - 1, reach - tallies[taker]) // 2
    margin = jnp.where((giver == order[0]) | (taker == order[0]) | (tallies[taker] == 0), 0, jnp.maximum(margin, 0))
    passed = jax.random.randint(jax.random.fold_in(own, 4), (amount // 2,), 0, 1 << 20) % (margin + 1)
    tallies = tallies.at[giver].add(-passed).at[taker].add(passed)
    members = jnp.searchsorted(jnp.cumsum(tallies), jnp.arange(rows * top), side="right").astype(jnp.int32)
    grid = members.reshape(top, rows).T
    grid = grid[jax.random.permutation(jax.random.fold_in(own, 1), rows)]
    offset_by = jax.random.randint(jax.random.fold_in(own, 2), (rows, 1), 0, top)
    return jnp.take_along_axis(grid, (jnp.arange(top)[None, :] + offset_by) % top, axis=1)


def shares(amount, total, limit, lean, full):
    weights = [(1 << 20) // math.isqrt(standing ** lean) + 1 for standing in range(1, amount + 1)]
    largest = limit if full else min(limit, max(-(-total // amount), total * weights[0] // sum(weights)))
    least = 1 if total - largest >= amount - 1 else 0
    holding, rest = [largest] + [least] * (amount - 1), total - largest - least * (amount - 1)
    while rest > 0:
        free = [i for i in range(1, amount) if holding[i] < largest] or [i for i in range(1, amount) if holding[i] < limit]
        whole, left = sum([weights[i] for i in free]), rest
        for i in free:
            extra = min(limit - holding[i], max(1, left * weights[i] // whole), rest)
            holding[i] = holding[i] + extra
            rest = rest - extra
    return np.array(holding)


def scatter_about(key, dims, deviation, most, cuts=(), kind=jnp.bfloat16):
    entries = deviation * jax.random.normal(key, dims, jnp.float32)
    if cuts:
        entries = entries * block_scale(key, dims, cuts, -0.22, 0.18)
    return jnp.clip(entries, -most, most).astype(kind)


def setup_inputs(seed: int = 0) -> dict:
    key_list = jax.random.split(jax.random.key(seed), 9)
    quot_owner_keys = jax.random.split(jax.random.fold_in(key_list[0], 1), TOKENS // TOK_DEV)
    quot_owner_turns = jax.random.permutation(jax.random.fold_in(key_list[0], 3), TOKENS // TOK_DEV)
    quot_owner = jax.vmap(lambda own, number: assign_block(jax.random.fold_in(key_list[0], 2), own, number, TOK_DEV, N_WIDE, 1, CAPQ, 2))(quot_owner_keys, quot_owner_turns).reshape((TOKENS, 1))
    quot_row = touch_ends(ranked(key_list[1], (TOKENS,), QPER, 2), jax.random.fold_in(key_list[1], 3), 0, QPER - 1).astype(jnp.int32)
    rem_owner = draw_rem_owner(jax.random.fold_in(key_list[8], 71), 0)
    rem_row = draw_rem_row(jax.random.fold_in(key_list[8], 71), 0)
    out_grad = scatter_about(key_list[4], (TOKENS, E), 1.0, 6.0, ((0, 512),))
    quot_table = draw_quot_table(jax.random.fold_in(key_list[8], 71), 0)
    quot_scale = jnp.clip(jnp.exp(math.log(0.02) - 2.30258502 * jax.random.uniform(key_list[6], (QROWS,), jnp.float32) ** block_scale(key_list[6], (QROWS,), ((0, 64),), -0.2, 0.2)), 0.002, 0.02)
    rem_table = scatter_about(key_list[7], (RROWS, E), 1.0, 4.0, ((0, 8),))
    return {"quot_owner": quot_owner, "quot_row": quot_row, "rem_owner": rem_owner, "rem_row": rem_row, "out_grad": out_grad, "quot_table": quot_table, "quot_scale": quot_scale, "rem_table": rem_table}


def reference(quot_owner, quot_row, rem_owner, rem_row, out_grad, quot_table, quot_scale, rem_table):
    quot_id = (quot_owner[:, 0] * (QROWS // N_WIDE) + quot_row).astype(jnp.int32)
    rem_id = (rem_owner[:, 0] * (RROWS // N_NARROW) + rem_row).astype(jnp.int32)
    dequant = (quot_table.astype(jnp.float32) * quot_scale[:, None]).astype(jnp.bfloat16)
    grads = out_grad.astype(jnp.float32)
    prod_q = (grads * rem_table[rem_id].astype(jnp.float32)).astype(jnp.bfloat16)
    prod_r = (grads * dequant[quot_id].astype(jnp.float32)).astype(jnp.bfloat16)
    grad_quot = jax.ops.segment_sum(prod_q.astype(jnp.float32), quot_id, num_segments=QROWS)
    grad_rem = jax.ops.segment_sum(prod_r.astype(jnp.float32), rem_id, num_segments=RROWS)
    return grad_quot, grad_rem.reshape(N_NARROW, RROWS // N_NARROW, E)
```

```python
import jax
import jax.numpy as jnp
from jax import lax
from jax.sharding import PartitionSpec as P

BLOCK_CAP = 2


def earlier_equal(keys):
    size = keys.shape[-1]
    before = jnp.arange(size)[None, :] < jnp.arange(size)[:, None]
    same = keys[..., :, None] == keys[..., None, :]
    return jnp.sum((same & before).astype(jnp.int32), axis=-1)


def slot_mask(slots, target):
    return jnp.arange(slots, dtype=jnp.int32)[:, None] == target[None, :]


def pack_ints(mask, values):
    return jnp.max(jnp.where(mask, values[None, :], -1), axis=1)


def select_rows(mask, values, contract=1):
    return lax.dot_general(
        mask.astype(jnp.bfloat16),
        values,
        (((contract,), (0,)), ((), ())),
        preferred_element_type=jnp.float32,
    )


def exchange(value, axis):
    return lax.all_to_all(value, axis, split_axis=0, concat_axis=0, tiled=True)


def on_device(
    quot_owner, quot_row, rem_owner, rem_row, out_grad, quot_table, quot_scale, rem_table
):
    wide_size = lax.axis_size("wide")
    narrow_size = lax.axis_size("narrow")
    tokens, width = out_grad.shape
    quot_slots = 2 * tokens // wide_size
    rem_slots = tokens // narrow_size
    block_slots = BLOCK_CAP * narrow_size
    quot_rows = quot_table.shape[0]
    rows_each = rem_table.shape[0] // wide_size
    quot_owner, rem_owner = quot_owner[:, 0], rem_owner[:, 0]

    rem_target = rem_owner * rem_slots + earlier_equal(rem_owner)
    rem_mask = slot_mask(tokens, rem_target)
    rem_ids = exchange(pack_ints(rem_mask, rem_row).reshape(narrow_size, rem_slots), "narrow")

    quot_target = quot_owner * quot_slots + earlier_equal(quot_owner)
    quot_mask = slot_mask(wide_size * quot_slots, quot_target)
    got_ids = exchange(
        pack_ints(quot_mask, quot_row).reshape(wide_size, quot_slots), "wide"
    ).reshape(-1)

    grads = out_grad.astype(jnp.float32)
    fetched = rem_table.at[rem_ids].get(mode="promise_in_bounds")
    returned = exchange(fetched, "narrow").reshape(-1, width)

    dequant = (quot_table.astype(jnp.float32) * quot_scale[:, None]).astype(jnp.bfloat16)
    quot_pick = slot_mask(quot_rows, got_ids)
    quot_fetched = select_rows(quot_pick, dequant, 0).astype(jnp.bfloat16)
    quot_back = exchange(quot_fetched.reshape(wide_size, quot_slots, width), "wide")

    rem_tok = select_rows(rem_mask, returned, 0)
    product = (grads * rem_tok).astype(jnp.bfloat16)
    got_prod = exchange(
        select_rows(quot_mask, product)
        .astype(jnp.bfloat16)
        .reshape(wide_size, quot_slots, width),
        "wide",
    ).reshape(-1, width)

    quot_tok = select_rows(quot_mask, quot_back.reshape(-1, width), 0)
    prod_r = (grads * quot_tok).astype(jnp.bfloat16)
    rem_prod = exchange(
        select_rows(rem_mask, prod_r)
        .astype(jnp.bfloat16)
        .reshape(narrow_size, rem_slots, width),
        "narrow",
    ).reshape(-1, width)

    block = rem_ids // rows_each
    peers = jnp.arange(narrow_size, dtype=jnp.int32)[:, None]
    block_target = block * block_slots + peers * BLOCK_CAP + earlier_equal(block)
    block_mask = slot_mask(wide_size * block_slots, block_target.reshape(-1))
    block_ids = exchange(
        pack_ints(block_mask, (rem_ids % rows_each).reshape(-1)).reshape(
            wide_size, block_slots
        ),
        "wide",
    ).reshape(-1)
    block_prod = exchange(
        select_rows(block_mask, rem_prod)
        .astype(jnp.bfloat16)
        .reshape(wide_size, block_slots, width),
        "wide",
    ).reshape(-1, width)

    partial = select_rows(quot_pick, got_prod).astype(jnp.bfloat16)
    parts = exchange(partial.reshape(narrow_size, -1, width), "narrow")
    share = jnp.sum(parts.astype(jnp.float32), axis=0).astype(jnp.bfloat16)
    copies = jnp.broadcast_to(share[None], (narrow_size,) + share.shape)
    grad_quot = exchange(copies, "narrow").reshape(-1, width).astype(jnp.float32)

    grad_rem = select_rows(slot_mask(rows_each, block_ids), block_prod)
    return (grad_quot, grad_rem[None])


def solution(mesh):
    placed = (
        P(("wide", "narrow"), None),
        P(("wide", "narrow")),
        P(("wide", "narrow"), None),
        P(("wide", "narrow")),
        P(("wide", "narrow"), None),
        P("wide", None),
        P("wide"),
        P("narrow", None),
    )
    return jax.shard_map(
        on_device,
        mesh=mesh,
        in_specs=placed,
        out_specs=(P("wide", None), P("narrow", "wide", None)),
        check_vma=False,
    )
```

```python
import functools

import jax
import jax.numpy as jnp
from jax import lax
from jax.experimental import pallas as pl
from jax.experimental.pallas import tpu as pltpu
from jax.sharding import PartitionSpec as P

BLOCK_CAP = 2


def earlier_equal(keys):
    size = keys.shape[-1]
    before = jnp.arange(size)[None, :] < jnp.arange(size)[:, None]
    same = keys[..., :, None] == keys[..., None, :]
    return jnp.sum((same & before).astype(jnp.int32), axis=-1)


def slot_mask(slots, target):
    return jnp.arange(slots, dtype=jnp.int32)[:, None] == target[None, :]


def pack_ints(mask, values):
    return jnp.max(jnp.where(mask, values[None, :], -1), axis=1)


def select_rows(mask, values, contract=1):
    return lax.dot_general(
        mask.astype(jnp.bfloat16),
        values,
        (((contract,), (0,)), ((), ())),
        preferred_element_type=jnp.float32,
    )


MESH = pl.DeviceIdType.MESH
AXES = ("wide", "narrow")


def meet_peers():
    barrier = pltpu.get_barrier_semaphore()
    count = 0
    for axis in AXES:
        size, me = lax.axis_size(axis), lax.axis_index(axis)

        def greet(step, carry, axis=axis, size=size, me=me):
            peer = lax.rem(me + step, size)
            pl.semaphore_signal(barrier, inc=1, device_id={axis: peer}, device_id_type=MESH)
            return carry

        lax.fori_loop(1, size, greet, 0)
        count += size - 1
    pl.semaphore_wait(barrier, count)


def send_all(axis, pick, dst, send_sem, recv_sem):
    size, me = lax.axis_size(axis), lax.axis_index(axis)

    def send(step, carry):
        peer = lax.rem(me + step, size)
        pltpu.make_async_remote_copy(
            src_ref=pick(peer),
            dst_ref=dst.at[me],
            send_sem=send_sem,
            recv_sem=recv_sem,
            device_id={axis: peer},
            device_id_type=MESH,
        ).start()
        return carry

    lax.fori_loop(1, size, send, 0)


def wait_all(axis, dst, send_sem, recv_sem):
    size, me = lax.axis_size(axis), lax.axis_index(axis)
    rest = dst.at[pl.ds(0, size - 1)]
    pltpu.make_async_remote_copy(
        src_ref=rest,
        dst_ref=rest,
        send_sem=send_sem,
        recv_sem=recv_sem,
        device_id={axis: lax.rem(me + 1, size)},
        device_id_type=MESH,
    ).wait()


def exchange_kernel(axes, *refs):
    count = len(axes)
    srcs, dsts = refs[:count], refs[count : 2 * count]
    send_sems, recv_sems, own_sems = refs[2 * count :]
    meet_peers()
    own = []
    for i, axis in enumerate(axes):
        src = srcs[i]
        send_all(axis, lambda peer, src=src: src.at[peer], dsts[i], send_sems.at[i], recv_sems.at[i])
    for i, axis in enumerate(axes):
        me = lax.axis_index(axis)
        copy = pltpu.make_async_copy(srcs[i].at[me], dsts[i].at[me], own_sems.at[i])
        copy.start()
        own.append(copy)
    for copy in own:
        copy.wait()
    for i, axis in enumerate(axes):
        wait_all(axis, dsts[i], send_sems.at[i], recv_sems.at[i])


def exchange(ident, *pairs):
    axes = tuple(axis for _, axis in pairs)
    values = [value for value, _ in pairs]
    return pl.pallas_call(
        functools.partial(exchange_kernel, axes),
        out_shape=[jax.ShapeDtypeStruct(value.shape, value.dtype) for value in values],
        in_specs=[pl.BlockSpec(memory_space=pl.ANY)] * len(values),
        out_specs=[pl.BlockSpec(memory_space=pl.ANY)] * len(values),
        scratch_shapes=[pltpu.SemaphoreType.DMA((len(values),))] * 3,
        compiler_params=pltpu.CompilerParams(collective_id=ident, has_side_effects=True),
    )(*values)


def finish_kernel(
    block_src, part_src, block_dst, copies, landed, share, send_sems, recv_sems, own_sems
):
    meet_peers()
    wide_me, me = lax.axis_index("wide"), lax.axis_index("narrow")
    send_all("narrow", lambda peer: part_src.at[peer], landed, send_sems.at[0], recv_sems.at[0])
    send_all("wide", lambda peer: block_src.at[peer], block_dst, send_sems.at[1], recv_sems.at[1])
    own_part = pltpu.make_async_copy(part_src.at[me], landed.at[me], own_sems.at[0])
    own_part.start()
    own_block = pltpu.make_async_copy(block_src.at[wide_me], block_dst.at[wide_me], own_sems.at[1])
    own_block.start()
    own_part.wait()
    wait_all("narrow", landed, send_sems.at[0], recv_sems.at[0])
    total = landed[0].astype(jnp.float32)
    for peer in range(1, landed.shape[0]):
        total = total + landed[peer].astype(jnp.float32)
    share[...] = total.astype(share.dtype)
    send_all("narrow", lambda peer: share, copies, send_sems.at[2], recv_sems.at[2])
    own_share = pltpu.make_async_copy(share, copies.at[me], own_sems.at[2])
    own_share.start()
    own_share.wait()
    own_block.wait()
    wait_all("wide", block_dst, send_sems.at[1], recv_sems.at[1])
    wait_all("narrow", copies, send_sems.at[2], recv_sems.at[2])


def finish(ident, block_prod, parts):
    any_space = pl.BlockSpec(memory_space=pl.ANY)
    return pl.pallas_call(
        finish_kernel,
        out_shape=[
            jax.ShapeDtypeStruct(block_prod.shape, block_prod.dtype),
            jax.ShapeDtypeStruct(parts.shape, parts.dtype),
        ],
        in_specs=[any_space] * 2,
        out_specs=[any_space] * 2,
        scratch_shapes=[
            pltpu.VMEM(parts.shape, parts.dtype),
            pltpu.VMEM(parts.shape[1:], parts.dtype),
        ]
        + [pltpu.SemaphoreType.DMA((3,))] * 3,
        compiler_params=pltpu.CompilerParams(collective_id=ident, has_side_effects=True),
    )(block_prod, parts)


def widen(ids):
    return jnp.pad(ids, ((0, 0), (0, 128 - ids.shape[1])), constant_values=-1)[:, None, :]


def on_device(
    quot_owner, quot_row, rem_owner, rem_row, out_grad, quot_table, quot_scale, rem_table
):
    wide_size = lax.axis_size("wide")
    narrow_size = lax.axis_size("narrow")
    tokens, width = out_grad.shape
    quot_slots = 2 * tokens // wide_size
    rem_slots = tokens // narrow_size
    block_slots = BLOCK_CAP * narrow_size
    quot_rows = quot_table.shape[0]
    rows_each = rem_table.shape[0] // wide_size
    quot_owner, rem_owner = quot_owner[:, 0], rem_owner[:, 0]

    rem_target = rem_owner * rem_slots + earlier_equal(rem_owner)
    rem_mask = slot_mask(tokens, rem_target)
    quot_target = quot_owner * quot_slots + earlier_equal(quot_owner)
    quot_mask = slot_mask(wide_size * quot_slots, quot_target)
    got_ids, rem_ids = exchange(
        0,
        (widen(pack_ints(quot_mask, quot_row).reshape(wide_size, quot_slots)), "wide"),
        (widen(pack_ints(rem_mask, rem_row).reshape(narrow_size, rem_slots)), "narrow"),
    )
    got_ids = got_ids[:, 0, :quot_slots].reshape(-1)
    rem_ids = rem_ids[:, 0, :rem_slots]

    grads = out_grad.astype(jnp.float32)
    dequant = (quot_table.astype(jnp.float32) * quot_scale[:, None]).astype(jnp.bfloat16)
    quot_pick = slot_mask(quot_rows, got_ids)
    quot_fetched = select_rows(quot_pick, dequant, 0).astype(jnp.bfloat16)
    rem_fetched = rem_table.at[rem_ids].get(mode="promise_in_bounds")
    block = rem_ids // rows_each
    peers = jnp.arange(narrow_size, dtype=jnp.int32)[:, None]
    block_target = block * block_slots + peers * BLOCK_CAP + earlier_equal(block)
    block_mask = slot_mask(wide_size * block_slots, block_target.reshape(-1))
    block_ids = pack_ints(block_mask, (rem_ids % rows_each).reshape(-1))

    quot_back, returned, block_ids = exchange(
        1,
        (quot_fetched.reshape(wide_size, quot_slots, width), "wide"),
        (rem_fetched, "narrow"),
        (widen(block_ids.reshape(wide_size, block_slots)), "wide"),
    )
    block_ids = block_ids[:, 0, :block_slots].reshape(-1)
    rem_tok = select_rows(rem_mask, returned.reshape(-1, width), 0)
    product = (grads * rem_tok).astype(jnp.bfloat16)
    quot_tok = select_rows(quot_mask, quot_back.reshape(-1, width), 0)
    prod_r = (grads * quot_tok).astype(jnp.bfloat16)
    got_prod, rem_prod = exchange(
        2,
        (
            select_rows(quot_mask, product)
            .astype(jnp.bfloat16)
            .reshape(wide_size, quot_slots, width),
            "wide",
        ),
        (
            select_rows(rem_mask, prod_r)
            .astype(jnp.bfloat16)
            .reshape(narrow_size, rem_slots, width),
            "narrow",
        ),
    )
    block_send = select_rows(block_mask, rem_prod.reshape(-1, width)).astype(jnp.bfloat16)
    partial = select_rows(quot_pick, got_prod.reshape(-1, width)).astype(jnp.bfloat16)
    block_prod, copies = finish(
        3,
        block_send.reshape(wide_size, block_slots, width),
        partial.reshape(narrow_size, -1, width),
    )
    grad_quot = copies.reshape(-1, width).astype(jnp.float32)
    grad_rem = select_rows(slot_mask(rows_each, block_ids), block_prod.reshape(-1, width))
    return (grad_quot, grad_rem[None])


def solution(mesh):
    placed = (
        P(("wide", "narrow"), None),
        P(("wide", "narrow")),
        P(("wide", "narrow"), None),
        P(("wide", "narrow")),
        P(("wide", "narrow"), None),
        P("wide", None),
        P("wide"),
        P("narrow", None),
    )
    return jax.shard_map(
        on_device,
        mesh=mesh,
        in_specs=placed,
        out_specs=(P("wide", None), P("narrow", "wide", None)),
        check_vma=False,
    )
```

```python
import jax
import jax.numpy as jnp
from jax import lax
from jax.experimental import pallas as pl
from jax.experimental.pallas import tpu as pltpu
from jax.sharding import PartitionSpec as P

BLOCK_CAP = 2


def earlier_equal(keys):
    size = keys.shape[-1]
    before = jnp.arange(size)[None, :] < jnp.arange(size)[:, None]
    same = keys[..., :, None] == keys[..., None, :]
    return jnp.sum((same & before).astype(jnp.int32), axis=-1)


def pack_ints(slots, target, values):
    mask = jnp.arange(slots, dtype=jnp.int32)[:, None] == target[None, :]
    return jnp.max(jnp.where(mask, values[None, :] + 1, 0), axis=1)


def spread(ids, place):
    count = ids.shape[1]
    lane = jnp.arange(LANES, dtype=jnp.int32)[None, :]
    tiled = jnp.tile(ids, (1, LANES // count))
    return jnp.where(lane // count == place % (LANES // count), tiled, 0)[:, None, :]


MESH = pl.DeviceIdType.MESH
AXES = ("wide", "narrow")
LANES = 128


def meet_peers():
    barrier = pltpu.get_barrier_semaphore()
    count = 0
    for axis in AXES:
        size, me = lax.axis_size(axis), lax.axis_index(axis)

        def greet(step, carry, axis=axis, size=size, me=me):
            peer = lax.rem(me + step, size)
            pl.semaphore_signal(barrier, inc=1, device_id={axis: peer}, device_id_type=MESH)
            return carry

        lax.fori_loop(1, size, greet, 0)
        count += size - 1
    pl.semaphore_wait(barrier, count)


def send_all(axis, pick, dst, send_sem, recv_sem):
    size, me = lax.axis_size(axis), lax.axis_index(axis)

    def send(step, carry):
        peer = lax.rem(me + step, size)
        pltpu.make_async_remote_copy(
            src_ref=pick(peer),
            dst_ref=dst.at[me],
            send_sem=send_sem,
            recv_sem=recv_sem,
            device_id={axis: peer},
            device_id_type=MESH,
        ).start()
        return carry

    lax.fori_loop(1, size, send, 0)


def arrivals(axis, dst, send_sem, recv_sem):
    size, me = lax.axis_size(axis), lax.axis_index(axis)
    rest = dst.at[pl.ds(0, size - 1)]
    return pltpu.make_async_remote_copy(
        src_ref=rest,
        dst_ref=rest,
        send_sem=send_sem,
        recv_sem=recv_sem,
        device_id={axis: lax.rem(me + 1, size)},
        device_id_type=MESH,
    )


def one_hot(left, right):
    return jnp.where(left == right, 1.0, 0.0).astype(jnp.bfloat16)


def dot(left, right):
    return jnp.dot(left, right, preferred_element_type=jnp.float32)


def iota(shape, dim):
    return lax.broadcasted_iota(jnp.int32, shape, dim)


def join_ids(landed, joined, groups):
    each = landed.shape[0] // groups
    for group in range(groups):
        row = landed[group * each]
        for peer in range(1, each):
            row = row + landed[group * each + peer]
        joined[group : group + 1, :] = row - 1
    values = joined[...]
    flipped = values.T
    row = jnp.concatenate([values[g : g + 1, :] for g in range(groups)], axis=1)
    col = jnp.concatenate([flipped[:, g : g + 1] for g in range(groups)], axis=0)
    return row, col


def fused_kernel(
    wide_ids_src,
    narrow_ids_src,
    targets_ref,
    grads_ref,
    table_ref,
    scale_ref,
    rem_ref,
    copies,
    grad_rem_ref,
    wide_ids,
    narrow_ids,
    block_ids_src,
    block_ids,
    joined,
    dequant,
    quot_src,
    quot_back,
    rows_src,
    rows_back,
    prod_src,
    prod_got,
    rem_src,
    rem_got,
    block_src,
    block_got,
    pick,
    block_mask,
    part_src,
    parts,
    share,
    send_sems,
    recv_sems,
    own_sem,
):
    wide_me, narrow_me = lax.axis_index("wide"), lax.axis_index("narrow")
    wide_size, narrow_size = wide_ids.shape[0], narrow_ids.shape[0]
    tokens, width = grads_ref.shape
    quot_slots, block_slots = quot_src.shape[1], block_src.shape[1]
    quot_total, block_total = wide_size * quot_slots, wide_size * block_slots
    rem_slots = rows_src.shape[1]
    rows_each = grad_rem_ref.shape[0]
    waits = []

    def ship(axis, src, dst):
        index = len(waits)
        me = wide_me if axis == "wide" else narrow_me
        send_all(axis, lambda peer: src.at[peer], dst, send_sems.at[index], recv_sems.at[index])
        dst[me] = src[me]
        wait = arrivals(axis, dst, send_sems.at[index], recv_sems.at[index])
        waits.append(wait)
        return wait

    joined[...] = jnp.zeros_like(joined)
    meet_peers()
    narrow_ids_wait = ship("narrow", narrow_ids_src, narrow_ids)
    wide_ids_wait = ship("wide", wide_ids_src, wide_ids)

    scales = scale_ref[...].T
    for group in range(scale_ref.shape[0]):
        part = pl.ds(group * LANES, LANES)
        dequant[part, :] = (
            table_ref[part, :].astype(jnp.float32) * scales[:, group : group + 1]
        ).astype(jnp.bfloat16)
    targets = targets_ref[...]
    flipped = targets.T
    quot_row, rem_row = targets[0:1, :], targets[1:2, :]
    quot_col, rem_col = flipped[:, 0:1], flipped[:, 1:2]

    narrow_ids_wait.wait_recv()
    id_row, id_col = join_ids(narrow_ids, joined, tokens // LANES)
    rem_rows = rem_ref.shape[0]
    rows_src[...] = (
        dot(one_hot(id_col, iota((tokens, rem_rows), 1)), rem_ref[...])
        .astype(jnp.bfloat16)
        .reshape(rows_src.shape)
    )
    rows_wait = ship("narrow", rows_src, rows_back)

    wide_ids_wait.wait_recv()
    got_row, got_col = join_ids(wide_ids, joined, quot_total // LANES)
    quot_rows = dequant.shape[0]
    quot_src[...] = (
        dot(one_hot(got_col, iota((quot_total, quot_rows), 1)), dequant[...])
        .astype(jnp.bfloat16)
        .reshape(quot_src.shape)
    )
    quot_wait = ship("wide", quot_src, quot_back)

    each = tokens // narrow_size
    row_block, col_block = id_row // rows_each, id_col // rows_each
    row_place, col_place = iota((1, tokens), 1), iota((tokens, 1), 0)
    alike = (col_block == row_block) & (col_place // each == row_place // each)
    row_rank = jnp.sum(
        jnp.where(alike & (col_place < row_place), 1.0, 0.0), axis=0, keepdims=True
    ).astype(jnp.int32)
    col_rank = jnp.sum(
        jnp.where(alike & (row_place < col_place), 1.0, 0.0), axis=1, keepdims=True
    ).astype(jnp.int32)
    row_slot = (row_place // each) * BLOCK_CAP + row_rank
    col_slot = (col_place // each) * BLOCK_CAP + col_rank
    lane = iota((1, LANES), 1)
    here = lane // block_slots == lax.rem(wide_me, LANES // block_slots)
    offsets = (id_col - col_block * rows_each + 1).astype(jnp.float32)
    spread_ids = jnp.where(
        (col_slot == lax.rem(lane, block_slots)) & here, offsets, 0.0
    ).astype(jnp.bfloat16)
    sent_ids = dot(one_hot(iota((wide_size, 1), 0), row_block), spread_ids).astype(jnp.int32)
    for dest in range(wide_size):
        block_ids_src[dest] = sent_ids[dest : dest + 1, :]
    block_ids_wait = ship("wide", block_ids_src, block_ids)
    block_mask[...] = one_hot(iota((block_total, 1), 0), row_block * block_slots + row_slot)
    pick[...] = one_hot(iota((quot_rows, 1), 0), got_row)

    rows_wait.wait_recv()
    grads = grads_ref[...].astype(jnp.float32)
    rem_tok = dot(
        one_hot(rem_col, iota((tokens, tokens), 1)), rows_back[...].reshape(tokens, width)
    )
    prod_src[...] = (
        dot(one_hot(iota((quot_total, 1), 0), quot_row), (grads * rem_tok).astype(jnp.bfloat16))
        .astype(jnp.bfloat16)
        .reshape(prod_src.shape)
    )
    prod_wait = ship("wide", prod_src, prod_got)

    quot_wait.wait_recv()
    quot_tok = dot(
        one_hot(quot_col, iota((tokens, quot_total), 1)),
        quot_back[...].reshape(quot_total, width),
    )
    rem_src[...] = (
        dot(one_hot(iota((tokens, 1), 0), rem_row), (grads * quot_tok).astype(jnp.bfloat16))
        .astype(jnp.bfloat16)
        .reshape(rem_src.shape)
    )
    rem_wait = ship("narrow", rem_src, rem_got)

    rem_wait.wait_recv()
    block_src[...] = (
        dot(block_mask[...], rem_got[...].reshape(tokens, width))
        .astype(jnp.bfloat16)
        .reshape(block_src.shape)
    )
    block_wait = ship("wide", block_src, block_got)

    prod_wait.wait_recv()
    part_src[...] = (
        dot(pick[...], prod_got[...].reshape(quot_total, width))
        .astype(jnp.bfloat16)
        .reshape(part_src.shape)
    )
    part_wait = ship("narrow", part_src, parts)

    part_wait.wait_recv()
    total = parts[0].astype(jnp.float32)
    for peer in range(1, narrow_size):
        total = total + parts[peer].astype(jnp.float32)
    share[...] = total.astype(jnp.bfloat16)
    index = len(waits)
    send_all("narrow", lambda peer: share, copies, send_sems.at[index], recv_sems.at[index])
    own = pltpu.make_async_copy(share, copies.at[narrow_me], own_sem)
    own.start()
    copies_wait = arrivals("narrow", copies, send_sems.at[index], recv_sems.at[index])
    waits.append(copies_wait)

    block_ids_wait.wait_recv()
    last_row, _ = join_ids(block_ids, joined, block_total // LANES)
    last_mask = one_hot(iota((rows_each, 1), 0), last_row)
    block_wait.wait_recv()
    grad_rem_ref[...] = dot(last_mask, block_got[...].reshape(block_total, width))
    own.wait()
    copies_wait.wait_recv()
    for wait in waits:
        wait.wait_send()


def on_device(
    quot_owner, quot_row, rem_owner, rem_row, out_grad, quot_table, quot_scale, rem_table
):
    wide_size = lax.axis_size("wide")
    narrow_size = lax.axis_size("narrow")
    tokens, width = out_grad.shape
    quot_slots = 2 * tokens // wide_size
    rem_slots = tokens // narrow_size
    block_slots = BLOCK_CAP * narrow_size
    quot_rows = quot_table.shape[0]
    rows_each = rem_table.shape[0] // wide_size
    quot_owner, rem_owner = quot_owner[:, 0], rem_owner[:, 0]

    rem_target = rem_owner * rem_slots + earlier_equal(rem_owner)
    quot_target = quot_owner * quot_slots + earlier_equal(quot_owner)
    wide_ids = spread(
        pack_ints(wide_size * quot_slots, quot_target, quot_row).reshape(wide_size, quot_slots),
        lax.axis_index("wide"),
    )
    narrow_ids = spread(
        pack_ints(tokens, rem_target, rem_row).reshape(narrow_size, rem_slots),
        lax.axis_index("narrow"),
    )
    targets = jnp.zeros((8, tokens), jnp.int32).at[0].set(quot_target).at[1].set(rem_target)

    half = jnp.bfloat16
    wide_shape = pltpu.VMEM((wide_size, quot_slots, width), half)
    narrow_shape = pltpu.VMEM((narrow_size, rem_slots, width), half)
    block_shape = pltpu.VMEM((wide_size, block_slots, width), half)
    part = (narrow_size, quot_rows // narrow_size, width)
    whole = pl.BlockSpec(memory_space=pltpu.VMEM)
    copies, grad_rem = pl.pallas_call(
        fused_kernel,
        out_shape=[
            jax.ShapeDtypeStruct(part, half),
            jax.ShapeDtypeStruct((rows_each, width), jnp.float32),
        ],
        in_specs=[whole] * 7,
        out_specs=[pl.BlockSpec(memory_space=pl.ANY), whole],
        scratch_shapes=[
            pltpu.VMEM(wide_ids.shape, jnp.int32),
            pltpu.VMEM(narrow_ids.shape, jnp.int32),
            pltpu.VMEM(wide_ids.shape, jnp.int32),
            pltpu.VMEM(wide_ids.shape, jnp.int32),
            pltpu.VMEM((8, LANES), jnp.int32),
            pltpu.VMEM((quot_rows, width), half),
            wide_shape,
            wide_shape,
            narrow_shape,
            narrow_shape,
            wide_shape,
            wide_shape,
            narrow_shape,
            narrow_shape,
            block_shape,
            block_shape,
            pltpu.VMEM((quot_rows, wide_size * quot_slots), half),
            pltpu.VMEM((wide_size * block_slots, tokens), half),
            pltpu.VMEM(part, half),
            pltpu.VMEM(part, half),
            pltpu.VMEM(part[1:], half),
            pltpu.SemaphoreType.DMA((10,)),
            pltpu.SemaphoreType.DMA((10,)),
            pltpu.SemaphoreType.DMA,
        ],
        compiler_params=pltpu.CompilerParams(collective_id=0, has_side_effects=True),
    )(
        wide_ids,
        narrow_ids,
        targets,
        out_grad,
        quot_table,
        quot_scale.reshape(-1, LANES),
        rem_table,
    )
    return (copies.reshape(-1, width).astype(jnp.float32), grad_rem[None])


def solution(mesh):
    placed = (
        P(("wide", "narrow"), None),
        P(("wide", "narrow")),
        P(("wide", "narrow"), None),
        P(("wide", "narrow")),
        P(("wide", "narrow"), None),
        P("wide", None),
        P("wide"),
        P("narrow", None),
    )
    return jax.shard_map(
        on_device,
        mesh=mesh,
        in_specs=placed,
        out_specs=(P("wide", None), P("narrow", "wide", None)),
        check_vma=False,
    )
```

```python
import jax
import jax.numpy as jnp
from jax import lax
from jax.experimental import pallas as pl
from jax.experimental.pallas import tpu as pltpu
from jax.sharding import PartitionSpec as P

BLOCK_CAP = 2


MESH = pl.DeviceIdType.MESH
AXES = ("wide", "narrow")
LANES = 128
PIECES = 4


def greet_peers():
    barrier = pltpu.get_barrier_semaphore()
    count = 0
    for axis in AXES:
        size, me = lax.axis_size(axis), lax.axis_index(axis)

        def greet(step, carry, axis=axis, size=size, me=me):
            peer = lax.rem(me + step, size)
            pl.semaphore_signal(barrier, inc=1, device_id={axis: peer}, device_id_type=MESH)
            return carry

        lax.fori_loop(1, size, greet, 0)
        count += size - 1
    return barrier, count


def send_all(axis, pick, dst, send_sem, recv_sem, land=lambda dst, me: dst.at[me]):
    size, me = lax.axis_size(axis), lax.axis_index(axis)

    def send(step, carry):
        peer = lax.rem(me + step, size)
        pltpu.make_async_remote_copy(
            src_ref=pick(peer),
            dst_ref=land(dst, me),
            send_sem=send_sem,
            recv_sem=recv_sem,
            device_id={axis: peer},
            device_id_type=MESH,
        ).start()
        return carry

    lax.fori_loop(1, size, send, 0)


def arrivals(axis, dst, send_sem, recv_sem, land=lambda dst, rows: dst.at[rows]):
    size, me = lax.axis_size(axis), lax.axis_index(axis)
    rest = land(dst, pl.ds(0, size - 1))
    return pltpu.make_async_remote_copy(
        src_ref=rest,
        dst_ref=rest,
        send_sem=send_sem,
        recv_sem=recv_sem,
        device_id={axis: lax.rem(me + 1, size)},
        device_id_type=MESH,
    )


def one_hot(left, right):
    return jnp.where(left == right, 1.0, 0.0).astype(jnp.bfloat16)


def dot(left, right):
    return jnp.dot(left, right, preferred_element_type=jnp.float32)


def iota(shape, dim):
    return lax.broadcasted_iota(jnp.int32, shape, dim)


def ranks(alike):
    size = alike.shape[0]
    rows, cols = iota((1, size), 1), iota((size, 1), 0)
    row_rank = jnp.sum(jnp.where(alike & (cols < rows), 1.0, 0.0), axis=0, keepdims=True)
    col_rank = jnp.sum(jnp.where(alike & (rows < cols), 1.0, 0.0), axis=1, keepdims=True)
    return row_rank.astype(jnp.int32), col_rank.astype(jnp.int32)


def spread_ids(dests, dest_row, count, place, slot_col, value_col):
    lane = iota((1, LANES), 1)
    here = lane // count == lax.rem(place, LANES // count)
    spot = (slot_col == lax.rem(lane, count)) & here
    mask = one_hot(iota((dests, 1), 0), dest_row)
    value = value_col + 1
    high = value // 64

    def gather(digit):
        return dot(mask, jnp.where(spot, digit.astype(jnp.float32), 0.0).astype(jnp.bfloat16))

    return (gather(high) * 64.0 + gather(value - high * 64)).astype(jnp.int32)


def store_rows(dst, values):
    for row in range(dst.shape[0]):
        dst[row] = values[row : row + 1, :]


def join_ids(landed, joined, groups):
    each = landed.shape[0] // groups
    for group in range(groups):
        row = landed[group * each]
        for peer in range(1, each):
            row = row + landed[group * each + peer]
        joined[group : group + 1, :] = row - 1
    values = joined[...]
    flipped = values.T
    row = jnp.concatenate([values[g : g + 1, :] for g in range(groups)], axis=1)
    col = jnp.concatenate([flipped[:, g : g + 1] for g in range(groups)], axis=0)
    return row, col


def fused_kernel(
    quot_owner_ref,
    quot_row_ref,
    rem_owner_ref,
    rem_row_ref,
    grads_ref,
    table_ref,
    scale_ref,
    rem_ref,
    copies,
    grad_rem_ref,
    facts,
    wide_ids_src,
    narrow_ids_src,
    wide_ids,
    narrow_ids,
    block_ids_src,
    block_ids,
    joined,
    dequant,
    quot_src,
    quot_back,
    rows_src,
    rows_back,
    prod_src,
    prod_got,
    rem_src,
    rem_got,
    block_src,
    block_got,
    pick,
    block_mask,
    part_src,
    parts,
    share,
    send_sems,
    recv_sems,
    own_sems,
):
    wide_me, narrow_me = lax.axis_index("wide"), lax.axis_index("narrow")
    wide_size, narrow_size = wide_ids.shape[0], narrow_ids.shape[0]
    tokens, width = grads_ref.shape
    quot_slots, block_slots = quot_src.shape[1], block_src.shape[1]
    quot_total, block_total = wide_size * quot_slots, wide_size * block_slots
    rem_slots = rows_src.shape[1]
    rows_each = grad_rem_ref.shape[0]
    waits = []

    def ship(axis, src, dst):
        index = len(waits)
        me = wide_me if axis == "wide" else narrow_me
        send_all(axis, lambda peer: src.at[peer], dst, send_sems.at[index], recv_sems.at[index])
        dst[me] = src[me]
        wait = arrivals(axis, dst, send_sems.at[index], recv_sems.at[index])
        waits.append(wait)
        return wait

    barrier, greeted = greet_peers()
    joined[...] = jnp.zeros_like(joined)
    facts[...] = jnp.zeros_like(facts)
    inputs = (quot_owner_ref, quot_row_ref, rem_owner_ref, rem_row_ref)
    for row, ref in enumerate(inputs):
        facts[row : row + 1, :] = ref[...]
    flipped = facts[...].T
    quot_owner, rem_owner = quot_owner_ref[...], rem_owner_ref[...]
    quot_owner_col, quot_value = flipped[:, 0:1], flipped[:, 1:2]
    rem_owner_col, rem_value = flipped[:, 2:3], flipped[:, 3:4]
    row_rank, col_rank = ranks(rem_owner_col == rem_owner)
    rem_row, rem_col = rem_owner * rem_slots + row_rank, rem_owner_col * rem_slots + col_rank
    store_rows(
        narrow_ids_src,
        spread_ids(narrow_size, rem_owner, rem_slots, narrow_me, col_rank, rem_value),
    )
    row_rank, col_rank = ranks(quot_owner_col == quot_owner)
    quot_row = quot_owner * quot_slots + row_rank
    quot_col = quot_owner_col * quot_slots + col_rank
    store_rows(
        wide_ids_src,
        spread_ids(wide_size, quot_owner, quot_slots, wide_me, col_rank, quot_value),
    )
    pl.semaphore_wait(barrier, greeted)
    narrow_ids_wait = ship("narrow", narrow_ids_src, narrow_ids)
    wide_ids_wait = ship("wide", wide_ids_src, wide_ids)

    scales = scale_ref[...].T
    for group in range(scale_ref.shape[0]):
        part = pl.ds(group * LANES, LANES)
        dequant[part, :] = (
            table_ref[part, :].astype(jnp.float32) * scales[:, group : group + 1]
        ).astype(jnp.bfloat16)
    narrow_ids_wait.wait_recv()
    id_row, id_col = join_ids(narrow_ids, joined, tokens // LANES)
    rem_rows = rem_ref.shape[0]
    rows_src[...] = (
        dot(one_hot(id_col, iota((tokens, rem_rows), 1)), rem_ref[...])
        .astype(jnp.bfloat16)
        .reshape(rows_src.shape)
    )
    rows_wait = ship("narrow", rows_src, rows_back)

    wide_ids_wait.wait_recv()
    got_row, got_col = join_ids(wide_ids, joined, quot_total // LANES)
    quot_rows = dequant.shape[0]
    quot_src[...] = (
        dot(one_hot(got_col, iota((quot_total, quot_rows), 1)), dequant[...])
        .astype(jnp.bfloat16)
        .reshape(quot_src.shape)
    )
    quot_wait = ship("wide", quot_src, quot_back)

    each = tokens // narrow_size
    row_block, col_block = id_row // rows_each, id_col // rows_each
    row_place, col_place = iota((1, tokens), 1), iota((tokens, 1), 0)
    alike = (col_block == row_block) & (col_place // each == row_place // each)
    row_rank, col_rank = ranks(alike)
    row_slot = (row_place // each) * BLOCK_CAP + row_rank
    col_slot = (col_place // each) * BLOCK_CAP + col_rank
    offsets = id_col - col_block * rows_each
    store_rows(
        block_ids_src,
        spread_ids(wide_size, row_block, block_slots, wide_me, col_slot, offsets),
    )
    block_ids_wait = ship("wide", block_ids_src, block_ids)
    block_mask[...] = one_hot(iota((block_total, 1), 0), row_block * block_slots + row_slot)
    pick[...] = one_hot(iota((quot_rows, 1), 0), got_row)

    rows_wait.wait_recv()
    grads = grads_ref[...].astype(jnp.float32)
    rem_tok = dot(
        one_hot(rem_col, iota((tokens, tokens), 1)), rows_back[...].reshape(tokens, width)
    )
    prod_src[...] = (
        dot(one_hot(iota((quot_total, 1), 0), quot_row), (grads * rem_tok).astype(jnp.bfloat16))
        .astype(jnp.bfloat16)
        .reshape(prod_src.shape)
    )
    prod_wait = ship("wide", prod_src, prod_got)

    quot_wait.wait_recv()
    quot_tok = dot(
        one_hot(quot_col, iota((tokens, quot_total), 1)),
        quot_back[...].reshape(quot_total, width),
    )
    rem_src[...] = (
        dot(one_hot(iota((tokens, 1), 0), rem_row), (grads * quot_tok).astype(jnp.bfloat16))
        .astype(jnp.bfloat16)
        .reshape(rem_src.shape)
    )
    rem_wait = ship("narrow", rem_src, rem_got)

    rem_wait.wait_recv()
    block_src[...] = (
        dot(block_mask[...], rem_got[...].reshape(tokens, width))
        .astype(jnp.bfloat16)
        .reshape(block_src.shape)
    )
    block_wait = ship("wide", block_src, block_got)

    prod_wait.wait_recv()
    part_src[...] = (
        dot(pick[...], prod_got[...].reshape(quot_total, width))
        .astype(jnp.bfloat16)
        .reshape(part_src.shape)
    )
    step = part_src.shape[1] // PIECES
    part_waits, copy_waits, owns = [], [], []
    for piece in range(PIECES):
        rows, index = pl.ds(piece * step, step), len(waits)

        def land(dst, where, rows=rows):
            return dst.at[where, rows]

        sems = send_sems.at[index], recv_sems.at[index]
        send_all("narrow", lambda peer: land(part_src, peer), parts, *sems, land)
        wait = arrivals("narrow", parts, *sems, land)
        part_waits.append(wait)
        waits.append(wait)
    parts[narrow_me] = part_src[narrow_me]
    for piece in range(PIECES):
        rows, index = pl.ds(piece * step, step), len(waits)

        def land(dst, where, rows=rows):
            return dst.at[where, rows]

        part_waits[piece].wait_recv()
        total = parts[0, rows, :].astype(jnp.float32)
        for peer in range(1, narrow_size):
            total = total + parts[peer, rows, :].astype(jnp.float32)
        share[rows, :] = total.astype(jnp.bfloat16)
        sems = send_sems.at[index], recv_sems.at[index]
        send_all("narrow", lambda peer: share.at[rows], copies, *sems, land)
        own = pltpu.make_async_copy(share.at[rows], land(copies, narrow_me), own_sems.at[piece])
        own.start()
        owns.append(own)
        wait = arrivals("narrow", copies, *sems, land)
        copy_waits.append(wait)
        waits.append(wait)

    block_ids_wait.wait_recv()
    last_row, _ = join_ids(block_ids, joined, block_total // LANES)
    last_mask = one_hot(iota((rows_each, 1), 0), last_row)
    block_wait.wait_recv()
    grad_rem_ref[...] = dot(last_mask, block_got[...].reshape(block_total, width))
    for own in owns:
        own.wait()
    for wait in copy_waits:
        wait.wait_recv()
    for wait in waits:
        wait.wait_send()


def on_device(
    quot_owner, quot_row, rem_owner, rem_row, out_grad, quot_table, quot_scale, rem_table
):
    wide_size = lax.axis_size("wide")
    narrow_size = lax.axis_size("narrow")
    tokens, width = out_grad.shape
    quot_slots = 2 * tokens // wide_size
    rem_slots = tokens // narrow_size
    block_slots = BLOCK_CAP * narrow_size
    quot_rows = quot_table.shape[0]
    rows_each = rem_table.shape[0] // wide_size
    half = jnp.bfloat16
    wide_ids = pltpu.VMEM((wide_size, 1, LANES), jnp.int32)
    narrow_ids = pltpu.VMEM((narrow_size, 1, LANES), jnp.int32)
    wide_shape = pltpu.VMEM((wide_size, quot_slots, width), half)
    narrow_shape = pltpu.VMEM((narrow_size, rem_slots, width), half)
    block_shape = pltpu.VMEM((wide_size, block_slots, width), half)
    part = (narrow_size, quot_rows // narrow_size, width)
    whole = pl.BlockSpec(memory_space=pltpu.VMEM)
    copies, grad_rem = pl.pallas_call(
        fused_kernel,
        out_shape=[
            jax.ShapeDtypeStruct(part, half),
            jax.ShapeDtypeStruct((rows_each, width), jnp.float32),
        ],
        in_specs=[whole] * 8,
        out_specs=[pl.BlockSpec(memory_space=pl.ANY), whole],
        scratch_shapes=[
            pltpu.VMEM((8, tokens), jnp.int32),
            wide_ids,
            narrow_ids,
            wide_ids,
            narrow_ids,
            wide_ids,
            wide_ids,
            pltpu.VMEM((8, LANES), jnp.int32),
            pltpu.VMEM((quot_rows, width), half),
            wide_shape,
            wide_shape,
            narrow_shape,
            narrow_shape,
            wide_shape,
            wide_shape,
            narrow_shape,
            narrow_shape,
            block_shape,
            block_shape,
            pltpu.VMEM((quot_rows, wide_size * quot_slots), half),
            pltpu.VMEM((wide_size * block_slots, tokens), half),
            pltpu.VMEM(part, half),
            pltpu.VMEM(part, half),
            pltpu.VMEM(part[1:], half),
            pltpu.SemaphoreType.DMA((8 + 2 * PIECES,)),
            pltpu.SemaphoreType.DMA((8 + 2 * PIECES,)),
            pltpu.SemaphoreType.DMA((PIECES,)),
        ],
        compiler_params=pltpu.CompilerParams(collective_id=0, has_side_effects=True),
    )(
        quot_owner.reshape(1, -1),
        quot_row.reshape(1, -1),
        rem_owner.reshape(1, -1),
        rem_row.reshape(1, -1),
        out_grad,
        quot_table,
        quot_scale.reshape(-1, LANES),
        rem_table,
    )
    return (copies.reshape(-1, width).astype(jnp.float32), grad_rem[None])


def solution(mesh):
    placed = (
        P(("wide", "narrow"), None),
        P(("wide", "narrow")),
        P(("wide", "narrow"), None),
        P(("wide", "narrow")),
        P(("wide", "narrow"), None),
        P("wide", None),
        P("wide"),
        P("narrow", None),
    )
    return jax.shard_map(
        on_device,
        mesh=mesh,
        in_specs=placed,
        out_specs=(P("wide", None), P("narrow", "wide", None)),
        check_vma=False,
    )
```

```python
import jax
import jax.numpy as jnp
from jax import lax
from jax.experimental import pallas as pl
from jax.experimental.pallas import tpu as pltpu
from jax.sharding import PartitionSpec as P

BLOCK_CAP = 2


MESH = pl.DeviceIdType.MESH
AXES = ("wide", "narrow")
LANES = 128
PIECES = 2


def greet_peers():
    barrier = pltpu.get_barrier_semaphore()
    count = 0
    for axis in AXES:
        size, me = lax.axis_size(axis), lax.axis_index(axis)

        def greet(step, carry, axis=axis, size=size, me=me):
            peer = lax.rem(me + step, size)
            pl.semaphore_signal(barrier, inc=1, device_id={axis: peer}, device_id_type=MESH)
            return carry

        lax.fori_loop(1, size, greet, 0)
        count += size - 1
    return barrier, count


def send_all(axis, pick, dst, send_sem, recv_sem, land=lambda dst, me: dst.at[me]):
    size, me = lax.axis_size(axis), lax.axis_index(axis)

    def send(step, carry):
        peer = lax.rem(me + step, size)
        pltpu.make_async_remote_copy(
            src_ref=pick(peer),
            dst_ref=land(dst, me),
            send_sem=send_sem,
            recv_sem=recv_sem,
            device_id={axis: peer},
            device_id_type=MESH,
        ).start()
        return carry

    lax.fori_loop(1, size, send, 0)


def arrivals(axis, dst, send_sem, recv_sem, land=lambda dst, rows: dst.at[rows]):
    size, me = lax.axis_size(axis), lax.axis_index(axis)
    rest = land(dst, pl.ds(0, size - 1))
    return pltpu.make_async_remote_copy(
        src_ref=rest,
        dst_ref=rest,
        send_sem=send_sem,
        recv_sem=recv_sem,
        device_id={axis: lax.rem(me + 1, size)},
        device_id_type=MESH,
    )


def one_hot(left, right):
    return jnp.where(left == right, 1.0, 0.0).astype(jnp.bfloat16)


def dot(left, right):
    return jnp.dot(left, right, preferred_element_type=jnp.float32)


def iota(shape, dim):
    return lax.broadcasted_iota(jnp.int32, shape, dim)


def ranks(alike):
    size = alike.shape[0]
    rows, cols = iota((1, size), 1), iota((size, 1), 0)
    row_rank = jnp.sum(jnp.where(alike & (cols < rows), 1.0, 0.0), axis=0, keepdims=True)
    col_rank = jnp.sum(jnp.where(alike & (rows < cols), 1.0, 0.0), axis=1, keepdims=True)
    return row_rank.astype(jnp.int32), col_rank.astype(jnp.int32)


def spread_ids(dests, dest_row, count, place, slot_col, value_col):
    lane = iota((1, LANES), 1)
    here = lane // count == lax.rem(place, LANES // count)
    spot = (slot_col == lax.rem(lane, count)) & here
    mask = one_hot(iota((dests, 1), 0), dest_row)
    value = value_col + 1
    high = value // 64

    def gather(digit):
        return dot(mask, jnp.where(spot, digit.astype(jnp.float32), 0.0).astype(jnp.bfloat16))

    return (gather(high) * 64.0 + gather(value - high * 64)).astype(jnp.int32)


def store_rows(dst, values):
    for row in range(dst.shape[0]):
        dst[row] = values[row : row + 1, :]


def join_ids(landed, joined, groups):
    each = landed.shape[0] // groups
    for group in range(groups):
        row = landed[group * each]
        for peer in range(1, each):
            row = row + landed[group * each + peer]
        joined[group : group + 1, :] = row - 1
    values = joined[...]
    flipped = values.T
    row = jnp.concatenate([values[g : g + 1, :] for g in range(groups)], axis=1)
    col = jnp.concatenate([flipped[:, g : g + 1] for g in range(groups)], axis=0)
    return row, col


def fused_kernel(
    quot_owner_ref,
    quot_row_ref,
    rem_owner_ref,
    rem_row_ref,
    grads_src,
    table_src,
    scale_ref,
    table_rem,
    copies_left,
    copies_right,
    grad_rem_ref,
    grads_ref,
    table_ref,
    rem_ref,
    facts,
    wide_ids_src,
    narrow_ids_src,
    wide_ids,
    narrow_ids,
    block_ids_src,
    block_ids,
    joined,
    dequant,
    quot_src,
    quot_back,
    rows_src,
    rows_back,
    prod_left,
    prod_right,
    got_left,
    got_right,
    rem_src,
    rem_got,
    block_src,
    block_got,
    pick,
    block_mask,
    part_left,
    part_right,
    parts_left,
    parts_right,
    share_left,
    share_right,
    send_sems,
    recv_sems,
    own_sems,
    load_sems,
):
    wide_me, narrow_me = lax.axis_index("wide"), lax.axis_index("narrow")
    wide_size, narrow_size = wide_ids.shape[0], narrow_ids.shape[0]
    tokens, width = grads_ref.shape
    quot_slots, block_slots = quot_src.shape[1], block_src.shape[1]
    quot_total, block_total = wide_size * quot_slots, wide_size * block_slots
    rem_slots = rows_src.shape[1]
    rows_each = grad_rem_ref.shape[0]
    waits = []

    def ship(axis, src, dst):
        index = len(waits)
        me = wide_me if axis == "wide" else narrow_me
        send_all(axis, lambda peer: src.at[peer], dst, send_sems.at[index], recv_sems.at[index])
        dst[me] = src[me]
        wait = arrivals(axis, dst, send_sems.at[index], recv_sems.at[index])
        waits.append(wait)
        return wait

    loads = []
    for index, pair in enumerate(
        ((table_rem, rem_ref), (table_src, table_ref), (grads_src, grads_ref))
    ):
        load = pltpu.make_async_copy(*pair, load_sems.at[index])
        load.start()
        loads.append(load)
    barrier, greeted = greet_peers()
    joined[...] = jnp.zeros_like(joined)
    facts[...] = jnp.zeros_like(facts)
    inputs = (quot_owner_ref, quot_row_ref, rem_owner_ref, rem_row_ref)
    for row, ref in enumerate(inputs):
        facts[row : row + 1, :] = ref[...]
    flipped = facts[...].T
    quot_owner, rem_owner = quot_owner_ref[...], rem_owner_ref[...]
    quot_owner_col, quot_value = flipped[:, 0:1], flipped[:, 1:2]
    rem_owner_col, rem_value = flipped[:, 2:3], flipped[:, 3:4]
    row_rank, col_rank = ranks(rem_owner_col == rem_owner)
    rem_row, rem_col = rem_owner * rem_slots + row_rank, rem_owner_col * rem_slots + col_rank
    store_rows(
        narrow_ids_src,
        spread_ids(narrow_size, rem_owner, rem_slots, narrow_me, col_rank, rem_value),
    )
    row_rank, col_rank = ranks(quot_owner_col == quot_owner)
    quot_row = quot_owner * quot_slots + row_rank
    quot_col = quot_owner_col * quot_slots + col_rank
    store_rows(
        wide_ids_src,
        spread_ids(wide_size, quot_owner, quot_slots, wide_me, col_rank, quot_value),
    )
    pl.semaphore_wait(barrier, greeted)
    narrow_ids_wait = ship("narrow", narrow_ids_src, narrow_ids)
    wide_ids_wait = ship("wide", wide_ids_src, wide_ids)

    for load in loads:
        load.wait()
    scales = scale_ref[...].T
    for group in range(scale_ref.shape[0]):
        part = pl.ds(group * LANES, LANES)
        dequant[part, :] = (
            table_ref[part, :].astype(jnp.float32) * scales[:, group : group + 1]
        ).astype(jnp.bfloat16)
    narrow_ids_wait.wait_recv()
    id_row, id_col = join_ids(narrow_ids, joined, tokens // LANES)
    rem_rows = rem_ref.shape[0]
    rows_src[...] = (
        dot(one_hot(id_col, iota((tokens, rem_rows), 1)), rem_ref[...])
        .astype(jnp.bfloat16)
        .reshape(rows_src.shape)
    )
    rows_wait = ship("narrow", rows_src, rows_back)

    wide_ids_wait.wait_recv()
    got_row, got_col = join_ids(wide_ids, joined, quot_total // LANES)
    quot_rows = dequant.shape[0]
    quot_src[...] = (
        dot(one_hot(got_col, iota((quot_total, quot_rows), 1)), dequant[...])
        .astype(jnp.bfloat16)
        .reshape(quot_src.shape)
    )
    quot_wait = ship("wide", quot_src, quot_back)

    each = tokens // narrow_size
    row_block, col_block = id_row // rows_each, id_col // rows_each
    row_place, col_place = iota((1, tokens), 1), iota((tokens, 1), 0)
    alike = (col_block == row_block) & (col_place // each == row_place // each)
    row_rank, col_rank = ranks(alike)
    row_slot = (row_place // each) * BLOCK_CAP + row_rank
    col_slot = (col_place // each) * BLOCK_CAP + col_rank
    offsets = id_col - col_block * rows_each
    store_rows(
        block_ids_src,
        spread_ids(wide_size, row_block, block_slots, wide_me, col_slot, offsets),
    )
    block_ids_wait = ship("wide", block_ids_src, block_ids)
    block_mask[...] = one_hot(iota((block_total, 1), 0), row_block * block_slots + row_slot)
    pick[...] = one_hot(iota((quot_rows, 1), 0), got_row)

    rows_wait.wait_recv()
    grads = grads_ref[...].astype(jnp.float32)
    rem_tok = dot(
        one_hot(rem_col, iota((tokens, tokens), 1)), rows_back[...].reshape(tokens, width)
    )
    half = width // 2
    packed = dot(
        one_hot(iota((quot_total, 1), 0), quot_row), (grads * rem_tok).astype(jnp.bfloat16)
    ).astype(jnp.bfloat16)
    prod_left[...] = packed[:, :half].reshape(prod_left.shape)
    left_wait = ship("wide", prod_left, got_left)
    prod_right[...] = packed[:, half:].reshape(prod_right.shape)
    right_wait = ship("wide", prod_right, got_right)

    quot_wait.wait_recv()
    quot_tok = dot(
        one_hot(quot_col, iota((tokens, quot_total), 1)),
        quot_back[...].reshape(quot_total, width),
    )
    rem_src[...] = (
        dot(one_hot(iota((tokens, 1), 0), rem_row), (grads * quot_tok).astype(jnp.bfloat16))
        .astype(jnp.bfloat16)
        .reshape(rem_src.shape)
    )
    rem_wait = ship("narrow", rem_src, rem_got)

    step = part_left.shape[1] // PIECES

    def piece_of(piece):
        rows = pl.ds(piece * step, step)
        return rows, lambda dst, where: dst.at[where, rows]

    def reduce_parts(got, part_src, parts):
        part_src[...] = (
            dot(pick[...], got[...].reshape(quot_total, half))
            .astype(jnp.bfloat16)
            .reshape(part_src.shape)
        )
        started = []
        for piece in range(PIECES):
            rows, land = piece_of(piece)
            sems = send_sems.at[len(waits)], recv_sems.at[len(waits)]
            send_all("narrow", lambda peer: land(part_src, peer), parts, *sems, land)
            started.append(arrivals("narrow", parts, *sems, land))
            waits.append(started[-1])
        parts[narrow_me] = part_src[narrow_me]
        return started

    owns, copy_waits = [], []

    def send_back(started, parts, share, copies):
        for piece in range(PIECES):
            rows, land = piece_of(piece)
            started[piece].wait_recv()
            total = parts[0, rows, :].astype(jnp.float32)
            for peer in range(1, narrow_size):
                total = total + parts[peer, rows, :].astype(jnp.float32)
            share[rows, :] = total.astype(jnp.bfloat16)
            sems = send_sems.at[len(waits)], recv_sems.at[len(waits)]
            send_all("narrow", lambda peer: share.at[rows], copies, *sems, land)
            own = pltpu.make_async_copy(
                share.at[rows], land(copies, narrow_me), own_sems.at[len(owns)]
            )
            own.start()
            owns.append(own)
            copy_waits.append(arrivals("narrow", copies, *sems, land))
            waits.append(copy_waits[-1])

    left_wait.wait_recv()
    left_started = reduce_parts(got_left, part_left, parts_left)

    rem_wait.wait_recv()
    block_src[...] = (
        dot(block_mask[...], rem_got[...].reshape(tokens, width))
        .astype(jnp.bfloat16)
        .reshape(block_src.shape)
    )
    block_wait = ship("wide", block_src, block_got)

    right_wait.wait_recv()
    right_started = reduce_parts(got_right, part_right, parts_right)
    send_back(left_started, parts_left, share_left, copies_left)
    send_back(right_started, parts_right, share_right, copies_right)

    block_ids_wait.wait_recv()
    last_row, _ = join_ids(block_ids, joined, block_total // LANES)
    last_mask = one_hot(iota((rows_each, 1), 0), last_row)
    block_wait.wait_recv()
    grad_rem_ref[...] = dot(last_mask, block_got[...].reshape(block_total, width))
    for own in owns:
        own.wait()
    for wait in copy_waits:
        wait.wait_recv()
    for wait in waits:
        wait.wait_send()


def output_kernel(left_ref, right_ref, rem_ref, quot_out, rem_out):
    half = left_ref.shape[1]
    quot_out[:, :half] = left_ref[...].astype(jnp.float32)
    quot_out[:, half:] = right_ref[...].astype(jnp.float32)
    rem_out[...] = rem_ref[...]


def write_outputs(left, right, rem):
    rows, half = left.shape
    tile = rows // 4
    side = pl.BlockSpec((tile, half), lambda i: (i, 0))
    rem_spec = pl.BlockSpec(rem.shape, lambda i: (0, 0))
    return pl.pallas_call(
        output_kernel,
        grid=(rows // tile,),
        out_shape=[
            jax.ShapeDtypeStruct((rows, 2 * half), jnp.float32),
            jax.ShapeDtypeStruct(rem.shape, jnp.float32),
        ],
        in_specs=[side, side, rem_spec],
        out_specs=[pl.BlockSpec((tile, 2 * half), lambda i: (i, 0)), rem_spec],
    )(left, right, rem)


def on_device(
    quot_owner, quot_row, rem_owner, rem_row, out_grad, quot_table, quot_scale, rem_table
):
    wide_size = lax.axis_size("wide")
    narrow_size = lax.axis_size("narrow")
    tokens, width = out_grad.shape
    quot_slots = 2 * tokens // wide_size
    rem_slots = tokens // narrow_size
    block_slots = BLOCK_CAP * narrow_size
    quot_rows = quot_table.shape[0]
    rows_each = rem_table.shape[0] // wide_size
    half = jnp.bfloat16
    wide_ids = pltpu.VMEM((wide_size, 1, LANES), jnp.int32)
    narrow_ids = pltpu.VMEM((narrow_size, 1, LANES), jnp.int32)
    wide_shape = pltpu.VMEM((wide_size, quot_slots, width), half)
    narrow_shape = pltpu.VMEM((narrow_size, rem_slots, width), half)
    block_shape = pltpu.VMEM((wide_size, block_slots, width), half)
    prod_shape = pltpu.VMEM((wide_size, quot_slots, width // 2), half)
    part = (narrow_size, quot_rows // narrow_size, width // 2)
    anywhere = pl.BlockSpec(memory_space=pl.ANY)
    whole = pl.BlockSpec(memory_space=pltpu.VMEM)
    left, right, grad_rem = pl.pallas_call(
        fused_kernel,
        out_shape=[
            jax.ShapeDtypeStruct(part, half),
            jax.ShapeDtypeStruct(part, half),
            jax.ShapeDtypeStruct((rows_each, width), jnp.float32),
        ],
        in_specs=[whole] * 4 + [anywhere, anywhere, whole, anywhere],
        out_specs=[anywhere, anywhere, whole],
        scratch_shapes=[
            pltpu.VMEM(out_grad.shape, half),
            pltpu.VMEM(quot_table.shape, half),
            pltpu.VMEM(rem_table.shape, half),
            pltpu.VMEM((8, tokens), jnp.int32),
            wide_ids,
            narrow_ids,
            wide_ids,
            narrow_ids,
            wide_ids,
            wide_ids,
            pltpu.VMEM((8, LANES), jnp.int32),
            pltpu.VMEM((quot_rows, width), half),
            wide_shape,
            wide_shape,
            narrow_shape,
            narrow_shape,
            prod_shape,
            prod_shape,
            prod_shape,
            prod_shape,
            narrow_shape,
            narrow_shape,
            block_shape,
            block_shape,
            pltpu.VMEM((quot_rows, wide_size * quot_slots), half),
            pltpu.VMEM((wide_size * block_slots, tokens), half),
            pltpu.VMEM(part, half),
            pltpu.VMEM(part, half),
            pltpu.VMEM(part, half),
            pltpu.VMEM(part, half),
            pltpu.VMEM(part[1:], half),
            pltpu.VMEM(part[1:], half),
            pltpu.SemaphoreType.DMA((9 + 4 * PIECES,)),
            pltpu.SemaphoreType.DMA((9 + 4 * PIECES,)),
            pltpu.SemaphoreType.DMA((2 * PIECES,)),
            pltpu.SemaphoreType.DMA((3,)),
        ],
        compiler_params=pltpu.CompilerParams(collective_id=0, has_side_effects=True),
    )(
        quot_owner.reshape(1, -1),
        quot_row.reshape(1, -1),
        rem_owner.reshape(1, -1),
        rem_row.reshape(1, -1),
        out_grad,
        quot_table,
        quot_scale.reshape(-1, LANES),
        rem_table,
    )
    grad_quot, grad_rem = write_outputs(
        left.reshape(quot_rows, -1), right.reshape(quot_rows, -1), grad_rem
    )
    return (grad_quot, grad_rem[None])


def solution(mesh):
    placed = (
        P(("wide", "narrow"), None),
        P(("wide", "narrow")),
        P(("wide", "narrow"), None),
        P(("wide", "narrow")),
        P(("wide", "narrow"), None),
        P("wide", None),
        P("wide"),
        P("narrow", None),
    )
    return jax.shard_map(
        on_device,
        mesh=mesh,
        in_specs=placed,
        out_specs=(P("wide", None), P("narrow", "wide", None)),
        check_vma=False,
    )
```

```python
import jax
import jax.numpy as jnp
from jax import lax
from jax.experimental import pallas as pl
from jax.experimental.pallas import tpu as pltpu
from jax.sharding import PartitionSpec as P

BLOCK_CAP = 2


MESH = pl.DeviceIdType.MESH
AXES = ("wide", "narrow")
LANES = 128
PIECES = 2
STRIDES = {"wide": 27, "narrow": 3}


def greet_peers():
    barrier = pltpu.get_barrier_semaphore()
    count = 0
    for axis in AXES:
        size, me = lax.axis_size(axis), lax.axis_index(axis)

        def greet(step, carry, axis=axis, size=size, me=me):
            peer = lax.rem(me + step, size)
            pl.semaphore_signal(barrier, inc=1, device_id={axis: peer}, device_id_type=MESH)
            return carry

        lax.fori_loop(1, size, greet, 0)
        count += size - 1
    return barrier, count


def send_all(axis, pick, dst, send_sem, recv_sem, land=lambda dst, me: dst.at[me]):
    size, me = lax.axis_size(axis), lax.axis_index(axis)

    def send(step, carry):
        peer = lax.rem(me + step * STRIDES[axis], size)
        pltpu.make_async_remote_copy(
            src_ref=pick(peer),
            dst_ref=land(dst, me),
            send_sem=send_sem,
            recv_sem=recv_sem,
            device_id={axis: peer},
            device_id_type=MESH,
        ).start()
        return carry

    lax.fori_loop(1, size, send, 0)


def arrivals(axis, dst, send_sem, recv_sem, land=lambda dst, rows: dst.at[rows]):
    size, me = lax.axis_size(axis), lax.axis_index(axis)
    rest = land(dst, pl.ds(0, size - 1))
    return pltpu.make_async_remote_copy(
        src_ref=rest,
        dst_ref=rest,
        send_sem=send_sem,
        recv_sem=recv_sem,
        device_id={axis: lax.rem(me + 1, size)},
        device_id_type=MESH,
    )


def one_hot(left, right):
    return jnp.where(left == right, 1.0, 0.0).astype(jnp.bfloat16)


def dot(left, right):
    return jnp.dot(left, right, preferred_element_type=jnp.float32)


def iota(shape, dim):
    return lax.broadcasted_iota(jnp.int32, shape, dim)


def ranks(alike):
    size = alike.shape[0]
    rows, cols = iota((1, size), 1), iota((size, 1), 0)
    row_rank = jnp.sum(jnp.where(alike & (cols < rows), 1.0, 0.0), axis=0, keepdims=True)
    col_rank = jnp.sum(jnp.where(alike & (rows < cols), 1.0, 0.0), axis=1, keepdims=True)
    return row_rank.astype(jnp.int32), col_rank.astype(jnp.int32)


def spread_ids(dests, dest_row, count, place, slot_col, value_col):
    lane = iota((1, LANES), 1)
    here = lane // count == lax.rem(place, LANES // count)
    spot = (slot_col == lax.rem(lane, count)) & here
    mask = one_hot(iota((dests, 1), 0), dest_row)
    value = value_col + 1
    high = value // 64

    def gather(digit):
        return dot(mask, jnp.where(spot, digit.astype(jnp.float32), 0.0).astype(jnp.bfloat16))

    return (gather(high) * 64.0 + gather(value - high * 64)).astype(jnp.int32)


def store_rows(dst, values):
    for row in range(dst.shape[0]):
        dst[row] = values[row : row + 1, :]


def join_ids(landed, joined, groups):
    each = landed.shape[0] // groups
    for group in range(groups):
        row = landed[group * each]
        for peer in range(1, each):
            row = row + landed[group * each + peer]
        joined[group : group + 1, :] = row - 1
    values = joined[...]
    flipped = values.T
    row = jnp.concatenate([values[g : g + 1, :] for g in range(groups)], axis=1)
    col = jnp.concatenate([flipped[:, g : g + 1] for g in range(groups)], axis=0)
    return row, col


def fused_kernel(
    quot_owner_ref,
    quot_row_ref,
    rem_owner_ref,
    rem_row_ref,
    grads_src,
    table_src,
    scale_ref,
    table_rem,
    copies_left,
    copies_right,
    grad_rem_ref,
    grads_ref,
    table_ref,
    rem_ref,
    facts,
    wide_ids_src,
    narrow_ids_src,
    wide_ids,
    narrow_ids,
    block_ids_src,
    block_ids,
    joined,
    dequant,
    quot_src,
    quot_back,
    rows_src,
    rows_back,
    prod_left,
    prod_right,
    got_left,
    got_right,
    rem_src,
    rem_got,
    block_src,
    block_got,
    pick,
    block_mask,
    part_left,
    part_right,
    parts_left,
    parts_right,
    share_left,
    share_right,
    send_sems,
    recv_sems,
    own_sems,
    load_sems,
):
    wide_me, narrow_me = lax.axis_index("wide"), lax.axis_index("narrow")
    wide_size, narrow_size = wide_ids.shape[0], narrow_ids.shape[0]
    tokens, width = grads_ref.shape
    quot_slots, block_slots = quot_src.shape[1], block_src.shape[1]
    quot_total, block_total = wide_size * quot_slots, wide_size * block_slots
    rem_slots = rows_src.shape[1]
    rows_each = grad_rem_ref.shape[0]
    waits = []

    def ship(axis, src, dst):
        index = len(waits)
        me = wide_me if axis == "wide" else narrow_me
        send_all(axis, lambda peer: src.at[peer], dst, send_sems.at[index], recv_sems.at[index])
        dst[me] = src[me]
        wait = arrivals(axis, dst, send_sems.at[index], recv_sems.at[index])
        waits.append(wait)
        return wait

    loads = []
    for index, pair in enumerate(
        ((table_rem, rem_ref), (table_src, table_ref), (grads_src, grads_ref))
    ):
        load = pltpu.make_async_copy(*pair, load_sems.at[index])
        load.start()
        loads.append(load)
    barrier, greeted = greet_peers()
    joined[...] = jnp.zeros_like(joined)
    facts[...] = jnp.zeros_like(facts)
    inputs = (quot_owner_ref, quot_row_ref, rem_owner_ref, rem_row_ref)
    for row, ref in enumerate(inputs):
        facts[row : row + 1, :] = ref[...]
    flipped = facts[...].T
    quot_owner, rem_owner = quot_owner_ref[...], rem_owner_ref[...]
    quot_owner_col, quot_value = flipped[:, 0:1], flipped[:, 1:2]
    rem_owner_col, rem_value = flipped[:, 2:3], flipped[:, 3:4]
    row_rank, col_rank = ranks(rem_owner_col == rem_owner)
    rem_row, rem_col = rem_owner * rem_slots + row_rank, rem_owner_col * rem_slots + col_rank
    store_rows(
        narrow_ids_src,
        spread_ids(narrow_size, rem_owner, rem_slots, narrow_me, col_rank, rem_value),
    )
    row_rank, col_rank = ranks(quot_owner_col == quot_owner)
    quot_row = quot_owner * quot_slots + row_rank
    quot_col = quot_owner_col * quot_slots + col_rank
    store_rows(
        wide_ids_src,
        spread_ids(wide_size, quot_owner, quot_slots, wide_me, col_rank, quot_value),
    )
    pl.semaphore_wait(barrier, greeted)
    narrow_ids_wait = ship("narrow", narrow_ids_src, narrow_ids)
    wide_ids_wait = ship("wide", wide_ids_src, wide_ids)

    for load in loads:
        load.wait()
    scales = scale_ref[...].T
    for group in range(scale_ref.shape[0]):
        part = pl.ds(group * LANES, LANES)
        dequant[part, :] = (
            table_ref[part, :].astype(jnp.float32) * scales[:, group : group + 1]
        ).astype(jnp.bfloat16)
    narrow_ids_wait.wait_recv()
    id_row, id_col = join_ids(narrow_ids, joined, tokens // LANES)
    rem_rows = rem_ref.shape[0]
    rows_src[...] = (
        dot(one_hot(id_col, iota((tokens, rem_rows), 1)), rem_ref[...])
        .astype(jnp.bfloat16)
        .reshape(rows_src.shape)
    )
    rows_wait = ship("narrow", rows_src, rows_back)

    wide_ids_wait.wait_recv()
    got_row, got_col = join_ids(wide_ids, joined, quot_total // LANES)
    quot_rows = dequant.shape[0]
    quot_src[...] = (
        dot(one_hot(got_col, iota((quot_total, quot_rows), 1)), dequant[...])
        .astype(jnp.bfloat16)
        .reshape(quot_src.shape)
    )
    quot_wait = ship("wide", quot_src, quot_back)

    each = tokens // narrow_size
    row_block, col_block = id_row // rows_each, id_col // rows_each
    row_place, col_place = iota((1, tokens), 1), iota((tokens, 1), 0)
    alike = (col_block == row_block) & (col_place // each == row_place // each)
    row_rank, col_rank = ranks(alike)
    row_slot = (row_place // each) * BLOCK_CAP + row_rank
    col_slot = (col_place // each) * BLOCK_CAP + col_rank
    offsets = id_col - col_block * rows_each
    store_rows(
        block_ids_src,
        spread_ids(wide_size, row_block, block_slots, wide_me, col_slot, offsets),
    )
    block_ids_wait = ship("wide", block_ids_src, block_ids)
    block_mask[...] = one_hot(iota((block_total, 1), 0), row_block * block_slots + row_slot)
    pick[...] = one_hot(iota((quot_rows, 1), 0), got_row)

    rows_wait.wait_recv()
    grads = grads_ref[...].astype(jnp.float32)
    rem_tok = dot(
        one_hot(rem_col, iota((tokens, tokens), 1)), rows_back[...].reshape(tokens, width)
    )
    half = width // 2
    packed = dot(
        one_hot(iota((quot_total, 1), 0), quot_row), (grads * rem_tok).astype(jnp.bfloat16)
    ).astype(jnp.bfloat16)
    prod_left[...] = packed[:, :half].reshape(prod_left.shape)
    left_wait = ship("wide", prod_left, got_left)
    prod_right[...] = packed[:, half:].reshape(prod_right.shape)
    right_wait = ship("wide", prod_right, got_right)

    quot_wait.wait_recv()
    quot_tok = dot(
        one_hot(quot_col, iota((tokens, quot_total), 1)),
        quot_back[...].reshape(quot_total, width),
    )
    rem_src[...] = (
        dot(one_hot(iota((tokens, 1), 0), rem_row), (grads * quot_tok).astype(jnp.bfloat16))
        .astype(jnp.bfloat16)
        .reshape(rem_src.shape)
    )
    rem_wait = ship("narrow", rem_src, rem_got)

    step = part_left.shape[1] // PIECES

    def piece_of(piece):
        rows = pl.ds(piece * step, step)
        return rows, lambda dst, where: dst.at[where, rows]

    def reduce_parts(got, part_src, parts):
        part_src[...] = (
            dot(pick[...], got[...].reshape(quot_total, half))
            .astype(jnp.bfloat16)
            .reshape(part_src.shape)
        )
        started = []
        for piece in range(PIECES):
            rows, land = piece_of(piece)
            sems = send_sems.at[len(waits)], recv_sems.at[len(waits)]
            send_all("narrow", lambda peer: land(part_src, peer), parts, *sems, land)
            started.append(arrivals("narrow", parts, *sems, land))
            waits.append(started[-1])
        parts[narrow_me] = part_src[narrow_me]
        return started

    owns, copy_waits = [], []

    def send_back(started, parts, share, copies):
        for piece in range(PIECES):
            rows, land = piece_of(piece)
            started[piece].wait_recv()
            total = parts[0, rows, :].astype(jnp.float32)
            for peer in range(1, narrow_size):
                total = total + parts[peer, rows, :].astype(jnp.float32)
            share[rows, :] = total.astype(jnp.bfloat16)
            sems = send_sems.at[len(waits)], recv_sems.at[len(waits)]
            send_all("narrow", lambda peer: share.at[rows], copies, *sems, land)
            own = pltpu.make_async_copy(
                share.at[rows], land(copies, narrow_me), own_sems.at[len(owns)]
            )
            own.start()
            owns.append(own)
            copy_waits.append(arrivals("narrow", copies, *sems, land))
            waits.append(copy_waits[-1])

    left_wait.wait_recv()
    left_started = reduce_parts(got_left, part_left, parts_left)

    rem_wait.wait_recv()
    block_src[...] = (
        dot(block_mask[...], rem_got[...].reshape(tokens, width))
        .astype(jnp.bfloat16)
        .reshape(block_src.shape)
    )
    block_wait = ship("wide", block_src, block_got)

    right_wait.wait_recv()
    right_started = reduce_parts(got_right, part_right, parts_right)
    send_back(left_started, parts_left, share_left, copies_left)
    send_back(right_started, parts_right, share_right, copies_right)

    block_ids_wait.wait_recv()
    last_row, _ = join_ids(block_ids, joined, block_total // LANES)
    last_mask = one_hot(iota((rows_each, 1), 0), last_row)
    block_wait.wait_recv()
    grad_rem_ref[...] = dot(last_mask, block_got[...].reshape(block_total, width))
    for own in owns:
        own.wait()
    for wait in copy_waits:
        wait.wait_recv()
    for wait in waits:
        wait.wait_send()


def output_kernel(left_ref, right_ref, rem_ref, quot_out, rem_out):
    half = left_ref.shape[1]
    quot_out[:, :half] = left_ref[...].astype(jnp.float32)
    quot_out[:, half:] = right_ref[...].astype(jnp.float32)
    rem_out[...] = rem_ref[...]


def write_outputs(left, right, rem):
    rows, half = left.shape
    tile = rows // 2
    side = pl.BlockSpec((tile, half), lambda i: (i, 0))
    rem_spec = pl.BlockSpec(rem.shape, lambda i: (0, 0))
    return pl.pallas_call(
        output_kernel,
        grid=(rows // tile,),
        out_shape=[
            jax.ShapeDtypeStruct((rows, 2 * half), jnp.float32),
            jax.ShapeDtypeStruct(rem.shape, jnp.float32),
        ],
        in_specs=[side, side, rem_spec],
        out_specs=[pl.BlockSpec((tile, 2 * half), lambda i: (i, 0)), rem_spec],
    )(left, right, rem)


def on_device(
    quot_owner, quot_row, rem_owner, rem_row, out_grad, quot_table, quot_scale, rem_table
):
    wide_size = lax.axis_size("wide")
    narrow_size = lax.axis_size("narrow")
    tokens, width = out_grad.shape
    quot_slots = 2 * tokens // wide_size
    rem_slots = tokens // narrow_size
    block_slots = BLOCK_CAP * narrow_size
    quot_rows = quot_table.shape[0]
    rows_each = rem_table.shape[0] // wide_size
    half = jnp.bfloat16
    wide_ids = pltpu.VMEM((wide_size, 1, LANES), jnp.int32)
    narrow_ids = pltpu.VMEM((narrow_size, 1, LANES), jnp.int32)
    wide_shape = pltpu.VMEM((wide_size, quot_slots, width), half)
    narrow_shape = pltpu.VMEM((narrow_size, rem_slots, width), half)
    block_shape = pltpu.VMEM((wide_size, block_slots, width), half)
    prod_shape = pltpu.VMEM((wide_size, quot_slots, width // 2), half)
    part = (narrow_size, quot_rows // narrow_size, width // 2)
    anywhere = pl.BlockSpec(memory_space=pl.ANY)
    whole = pl.BlockSpec(memory_space=pltpu.VMEM)
    left, right, grad_rem = pl.pallas_call(
        fused_kernel,
        out_shape=[
            jax.ShapeDtypeStruct(part, half),
            jax.ShapeDtypeStruct(part, half),
            jax.ShapeDtypeStruct((rows_each, width), jnp.float32),
        ],
        in_specs=[whole] * 4 + [anywhere, anywhere, whole, anywhere],
        out_specs=[anywhere, anywhere, whole],
        scratch_shapes=[
            pltpu.VMEM(out_grad.shape, half),
            pltpu.VMEM(quot_table.shape, half),
            pltpu.VMEM(rem_table.shape, half),
            pltpu.VMEM((8, tokens), jnp.int32),
            wide_ids,
            narrow_ids,
            wide_ids,
            narrow_ids,
            wide_ids,
            wide_ids,
            pltpu.VMEM((8, LANES), jnp.int32),
            pltpu.VMEM((quot_rows, width), half),
            wide_shape,
            wide_shape,
            narrow_shape,
            narrow_shape,
            prod_shape,
            prod_shape,
            prod_shape,
            prod_shape,
            narrow_shape,
            narrow_shape,
            block_shape,
            block_shape,
            pltpu.VMEM((quot_rows, wide_size * quot_slots), half),
            pltpu.VMEM((wide_size * block_slots, tokens), half),
            pltpu.VMEM(part, half),
            pltpu.VMEM(part, half),
            pltpu.VMEM(part, half),
            pltpu.VMEM(part, half),
            pltpu.VMEM(part[1:], half),
            pltpu.VMEM(part[1:], half),
            pltpu.SemaphoreType.DMA((9 + 4 * PIECES,)),
            pltpu.SemaphoreType.DMA((9 + 4 * PIECES,)),
            pltpu.SemaphoreType.DMA((2 * PIECES,)),
            pltpu.SemaphoreType.DMA((3,)),
        ],
        compiler_params=pltpu.CompilerParams(collective_id=0, has_side_effects=True),
    )(
        quot_owner.reshape(1, -1),
        quot_row.reshape(1, -1),
        rem_owner.reshape(1, -1),
        rem_row.reshape(1, -1),
        out_grad,
        quot_table,
        quot_scale.reshape(-1, LANES),
        rem_table,
    )
    grad_quot, grad_rem = write_outputs(
        left.reshape(quot_rows, -1), right.reshape(quot_rows, -1), grad_rem
    )
    return (grad_quot, grad_rem[None])


def solution(mesh):
    placed = (
        P(("wide", "narrow"), None),
        P(("wide", "narrow")),
        P(("wide", "narrow"), None),
        P(("wide", "narrow")),
        P(("wide", "narrow"), None),
        P("wide", None),
        P("wide"),
        P("narrow", None),
    )
    return jax.shard_map(
        on_device,
        mesh=mesh,
        in_specs=placed,
        out_specs=(P("wide", None), P("narrow", "wide", None)),
        check_vma=False,
    )
```
